32 devices in a mesh: dp: 8 (over z, x), ctx: 4 (over y, core).
Axes of the slice: x: 2, y: 2, z: 4, core: 2. Of those that a mesh axis runs over, the one named last changes fastest.
Arguments:
- inputs: bfloat16 [8, 2048, 768], P('dp', 'ctx'), may hold values from -6 to 6
- segments: int32 [8, 2048], P('dp'), may hold values from 0 to 34, as said below
- qkv_weight: bfloat16 [768, 2304], P(('dp', 'ctx')), may hold values from -0.21875 to 0.21875
- query_value_bias: bfloat16 [1536], P(('dp', 'ctx')), may hold values from -3 to 3
- output_weight: bfloat16 [768, 768], P(('dp', 'ctx')), may hold values from -1.75 to 1.75
- output_bias: bfloat16 [768], P(('dp', 'ctx')), may hold values from -3 to 3
- attention_gain: bfloat16 [768], P(('dp', 'ctx')), may hold values from 0.25 to 1.75
- attention_shift: bfloat16 [768], P(('dp', 'ctx')), may hold values from -2 to 2
- up_weight: bfloat16 [768, 3072], P(('dp', 'ctx')), may hold values from -0.21875 to 0.21875
- up_bias: bfloat16 [3072], P(('dp', 'ctx')), may hold values from -3 to 3
- down_weight: bfloat16 [3072, 768], P(('dp', 'ctx')), may hold values from -0.109375 to 0.109375
- down_bias: bfloat16 [768], P(('dp', 'ctx')), may hold values from -3 to 3
- final_gain: bfloat16 [768], P(('dp', 'ctx')), may hold values from 0.25 to 1.75
- final_shift: bfloat16 [768], P(('dp', 'ctx')), may hold values from -2 to 2
- cotangent: bfloat16 [8, 2048, 768], P('dp', 'ctx'), may hold values from -6 to 6
Outputs:
- output: bfloat16 [8, 2048, 768], P('dp', 'ctx')
- input_grad: float32 [8, 2048, 768], P('dp', 'ctx')
- qkv_weight_grad: float32 [768, 2304], P(('dp', 'ctx'))
- query_value_bias_grad: float32 [1536], P(('dp', 'ctx'))
- output_weight_grad: float32 [768, 768], P(('dp', 'ctx'))
- output_bias_grad: float32 [768], P(('dp', 'ctx'))
- attention_gain_grad: float32 [768], P(('dp', 'ctx'))
- attention_shift_grad: float32 [768], P(('dp', 'ctx'))
- up_weight_grad: float32 [768, 3072], P(('dp', 'ctx'))
- up_bias_grad: float32 [3072], P(('dp', 'ctx'))
- down_weight_grad: float32 [3072, 768], P(('dp', 'ctx'))
- down_bias_grad: float32 [768], P(('dp', 'ctx'))
- final_gain_grad: float32 [768], P(('dp', 'ctx'))
- final_shift_grad: float32 [768], P(('dp', 'ctx'))
The draws below stay inside these ranges and needn't reach their ends.
Inputs may be any that keep to these rules, and one draw needn't show every extreme that they name: `segments`: in each sequence, segment numbers count its whole documents from 1 in order of position; each document spans 60 to 800 positions; the positions after the last whole document, one or more, are 0. The first sequence is packed with documents of exactly 60 positions.
All inputs are finite; a program needn't handle non-finite values.
Results may differ from the reference program's by a relative error of at most 0.017.
Values may be sent and summed in bfloat16 or wider, within the bound.
No kernel may reach another device: no remote copies, remote signals or barrier semaphores. Data moves between devices by JAX's collectives and lax.ppermute only.
A program may use at most 128 MiB of HBM per device.

```python
import jax
import jax.numpy as jnp
from jax import lax

D = 768
HEADS = 12
HEAD_DIM = 64
FF = 3072
SEQ_LEN = 2048
DOC_MIN = 60
DOC_MAX = 800
SEQS = 8


def draw_segments(key, part):
    most_docs = SEQ_LEN // DOC_MIN + 1

    def one_row(row_key, row_number):
        drawn = jax.random.randint(row_key, (most_docs,), DOC_MIN, DOC_MAX + 1)
        lengths = jnp.where(row_number == 0, jnp.full((most_docs,), DOC_MIN, jnp.int32), drawn)
        doc_ends = jnp.cumsum(lengths)
        places = jnp.arange(SEQ_LEN)
        doc_index = jnp.sum((doc_ends[None, :] <= places[:, None]).astype(jnp.int32), axis=1)
        closing = jnp.take(doc_ends, doc_index)
        return jnp.where(closing < SEQ_LEN, doc_index + 1, 0).astype(jnp.int32)
    row_keys = jax.random.split(jax.random.fold_in(key, 7), SEQS)
    return jax.vmap(one_row)(row_keys, jnp.arange(SEQS, dtype=jnp.int32))


def block_scale(key, extent, cuts, least, largest):
    level = 1.0
    for axis_at, blocks in cuts:
        steps = jax.random.uniform(jax.random.fold_in(jax.random.fold_in(key, 6), axis_at), (blocks,), jnp.float32, least / len(cuts), largest / len(cuts))
        level = level * jnp.repeat(jnp.exp(steps), extent[axis_at] // blocks).reshape((-1,) + (1,) * (len(extent) - 1 - axis_at))
    return level


def gaussian(own_key, shape, scale, reach, pieces=(), kind=jnp.bfloat16):
    values = jax.random.normal(own_key, shape, jnp.float32) * scale
    if len(pieces) > 0:
        values = block_scale(own_key, shape, pieces, -0.22, 0.18) * values
    return jnp.clip(values, min=-reach, max=reach).astype(kind)


def setup_inputs(seed: int = 0) -> dict:
    keys = jax.random.split(jax.random.key(seed), 16)
    return {
        "inputs": gaussian(keys[0], (SEQS, SEQ_LEN, D), 1.0, 6.0, ((0, 8), (1, 4))),
        "segments": draw_segments(jax.random.fold_in(keys[15], 71), 0),
        "qkv_weight": gaussian(keys[2], (D, 3 * D), D ** -0.5, 0.21875, ((0, 32),)),
        "query_value_bias": gaussian(keys[3], (2 * D,), 0.5, 3.0, ((0, 32),)),
        "output_weight": gaussian(keys[4], (D, D), (D // 64) ** -0.5, 1.75, ((0, 32),)),
        "output_bias": gaussian(keys[5], (D,), 0.5, 3.0, ((0, 32),)),
        "attention_gain": jnp.clip(1.0 + 0.15 * jax.random.normal(keys[6], (D,), jnp.float32), 0.25, 1.75).astype(jnp.bfloat16),
        "attention_shift": gaussian(keys[7], (D,), 0.3, 2.0, ((0, 32),)),
        "up_weight": gaussian(keys[8], (D, FF), D ** -0.5, 0.21875, ((0, 32),)),
        "up_bias": gaussian(keys[9], (FF,), 0.5, 3.0, ((0, 32),)),
        "down_weight": gaussian(keys[10], (FF, D), FF ** -0.5, 0.109375, ((0, 32),)),
        "down_bias": gaussian(keys[11], (D,), 0.5, 3.0, ((0, 32),)),
        "final_gain": jnp.clip(1.0 + 0.15 * jax.random.normal(keys[12], (D,), jnp.float32), 0.25, 1.75).astype(jnp.bfloat16),
        "final_shift": gaussian(keys[13], (D,), 0.3, 2.0, ((0, 32),)),
        "cotangent": gaussian(keys[14], (SEQS, SEQ_LEN, D), 1.0, 6.0, ((0, 8), (1, 4))),
    }


@jax.custom_vjp
def low(v):
    return lax.optimization_barrier(v.astype(jnp.bfloat16)).astype(jnp.float32)

@jax.custom_vjp
def low_back(v):
    return v

def low_keep(v):
    return (low(v), None)

def low_pass(kept, grad):
    return (grad,)

def back_keep(v):
    return (v, None)

def back_low(kept, grad):
    return (low(grad),)
low.defvjp(low_keep, low_pass)
low_back.defvjp(back_keep, back_low)

def layer_norm(rows, gain, shift):
    center = lax.optimization_barrier(jnp.mean(rows, axis=-1, keepdims=True))
    centred = rows - center
    spread = lax.optimization_barrier(jnp.mean(centred * centred, axis=-1, keepdims=True))
    return centred * lax.rsqrt(spread + 1e-06) * gain + shift

def block_attention(query_block, query_seg, key_rows, value_rows, key_seg):
    scores = low_back(jnp.einsum('qhd,khd->qhk', query_block, key_rows, precision=lax.Precision.HIGHEST))
    allowed = (query_seg[:, None] == key_seg[None, :]) & (key_seg[None, :] > 0)
    masked = jnp.where(allowed[:, None, :], scores, -1000000000.0)
    row_top = jnp.maximum(lax.optimization_barrier(jnp.max(masked, axis=-1)), 0.0)
    weights = jnp.exp(masked - row_top[..., None])
    totals = lax.optimization_barrier(jnp.sum(weights, axis=-1))
    safe_total = jnp.where(query_seg[:, None] > 0, totals, 1.0)
    probs = low(weights / safe_total[..., None])
    return jnp.einsum('qhk,khd->qhd', probs, value_rows, precision=lax.Precision.HIGHEST)

def sequence_layer(params, states, seq_segments):
    qkv_w, qv_bias, out_w, out_bias, gain_one, shift_one, up_w, up_b, down_w, down_b, gain_two, shift_two = params
    zero_keys = jnp.zeros((D,), states.dtype)
    full_bias = jnp.concatenate([qv_bias[:D], zero_keys, qv_bias[D:]])
    qkv_rows = low_back(jnp.dot(low(states), qkv_w, precision=lax.Precision.HIGHEST) + full_bias)
    queries = low(qkv_rows[:, :D] * 0.125).reshape(SEQ_LEN, HEADS, HEAD_DIM)
    key_rows = low(qkv_rows[:, D:2 * D]).reshape(SEQ_LEN, HEADS, HEAD_DIM)
    value_rows = low(qkv_rows[:, 2 * D:]).reshape(SEQ_LEN, HEADS, HEAD_DIM)
    block_rows = 512 if SEQ_LEN % 512 == 0 else SEQ_LEN
    block_count = SEQ_LEN // block_rows
    query_blocks = queries.reshape(block_count, block_rows, HEADS, HEAD_DIM)
    seg_blocks = seq_segments.reshape(block_count, block_rows)

    def one_block(packed):
        return block_attention(packed[0], packed[1], key_rows, value_rows, seq_segments)
    attended = lax.map(jax.checkpoint(one_block), (query_blocks, seg_blocks)).reshape(SEQ_LEN, D)
    mixed = low_back(low(attended))
    branch = low_back(jnp.dot(mixed, out_w, precision=lax.Precision.HIGHEST) + out_bias)
    normed = layer_norm(states + branch, gain_one, shift_one)
    hidden_pre = low_back(jnp.dot(low(normed), up_w, precision=lax.Precision.HIGHEST) + up_b)
    hidden = low(jax.nn.gelu(hidden_pre, approximate=False))
    feed = low_back(jnp.dot(hidden, down_w, precision=lax.Precision.HIGHEST) + down_b)
    return layer_norm(normed + feed, gain_two, shift_two)

def reference(inputs, segments, qkv_weight, query_value_bias, output_weight, output_bias, attention_gain, attention_shift, up_weight, up_bias, down_weight, down_bias, final_gain, final_shift, cotangent):
    params = tuple((member.astype(jnp.float32) for member in (qkv_weight, query_value_bias, output_weight, output_bias, attention_gain, attention_shift, up_weight, up_bias, down_weight, down_bias, final_gain, final_shift)))

    def forward(states, *weights):

        def one_sequence(packed):
            return sequence_layer(weights, packed[0], packed[1])
        return lax.map(jax.checkpoint(one_sequence), (states, segments))
    result, pullback = jax.vjp(forward, inputs.astype(jnp.float32), *params)
    grads = pullback(cotangent.astype(jnp.float32))
    return (result.astype(jnp.bfloat16), grads[0], grads[1], grads[2], grads[3], grads[4], grads[5], grads[6], grads[7], grads[8], grads[9], grads[10], grads[11], grads[12])
```

```python
import jax
import jax.numpy as jnp
from jax import lax
from jax.sharding import PartitionSpec as P

HEADS = 12
HEAD_DIM = 64
LANES = 128

MASKED = -1000000000.0


def layer_norm(rows, gain, shift):
    center = jnp.mean(rows, axis=-1, keepdims=True)
    centred = rows - center
    spread = jnp.mean(centred * centred, axis=-1, keepdims=True)
    return centred * lax.rsqrt(spread + 1e-06) * gain + shift


def exact_gelu(values):
    return jax.nn.gelu(values, approximate=False)


def inner_rows(left, right):
    return lax.dot_general(
        left, right, (((0,), (0,)), ((), ())), preferred_element_type=jnp.float32
    )


def times_transpose(left, right):
    return lax.dot_general(
        left, right, (((1,), (1,)), ((), ())), preferred_element_type=jnp.float32
    )


def axis_bits(name):
    size = lax.axis_size(name)
    return [(name, 1 << k) for k in range(size.bit_length() - 1)]


def index_bits():
    return axis_bits("dp")[::-1] + axis_bits("ctx")[::-1]


def exchange_orders():
    dp, ctx = axis_bits("dp"), axis_bits("ctx")
    core, side, near, far = ctx[:1], ctx[1:], dp[:1], dp[1:]
    return (
        core + near + side + far,
        core + side + near + far,
        core + far[:1] + near + side + far[1:],
    )


def partner(value, bit):
    name, step = bit
    pairs = [(i, i ^ step) for i in range(lax.axis_size(name))]
    return lax.ppermute(value, name, pairs)


def own_bit(bit):
    name, step = bit
    return (lax.axis_index(name) // step) % 2


def gather_rows(shard, order, bits):
    rows, cols = shard.shape
    have = []
    held = shard
    for bit in order:
        theirs = partner(held, bit)
        place = sum(1 for other in have if bits.index(other) < bits.index(bit))
        shape = [1] * (held.ndim + 1)
        shape[place] = 2
        mine = jnp.arange(2).reshape(shape) == own_bit(bit)
        held = jnp.where(mine, jnp.expand_dims(held, place), jnp.expand_dims(theirs, place))
        have.append(bit)
    return held.reshape(rows << len(order), cols)


def scatter_rows(full, order, bits):
    rows, cols = full.shape
    have = list(bits)
    held = full.astype(jnp.bfloat16).reshape([2] * len(bits) + [rows >> len(bits), cols])
    for bit in order:
        place = have.index(bit)
        mine = own_bit(bit)
        keep = lax.dynamic_index_in_dim(held, mine, place, keepdims=False)
        send = lax.dynamic_index_in_dim(held, 1 - mine, place, keepdims=False)
        total = keep.astype(jnp.float32) + partner(send, bit).astype(jnp.float32)
        have.remove(bit)
        held = total.astype(jnp.bfloat16) if have else total
    return held


def masked_scores(queries, block_keys, query_seg, key_seg):
    scores = jnp.einsum("qhd,khd->qhk", queries, block_keys, preferred_element_type=jnp.float32)
    allowed = (query_seg[:, None, None] == key_seg[None, None, :]) & (key_seg[None, None, :] > 0)
    return jnp.where(allowed, scores, MASKED)


def key_block(rows, begin, size):
    return lax.dynamic_slice_in_dim(rows, begin, size, 0).reshape(size, HEADS, HEAD_DIM)


def attention_forward(queries, key_rows, value_rows, query_seg, seg_row):
    group = queries.shape[0]
    block_size = 512
    heads_in = queries.reshape(group, HEADS, HEAD_DIM)

    def forward_one_block(state, block_index):
        running, row_max, row_sum = state
        begin = block_index * block_size
        key_seg = lax.dynamic_slice_in_dim(seg_row, begin, block_size, 0)
        masked = masked_scores(heads_in, key_block(key_rows, begin, block_size), query_seg, key_seg)
        new_max = jnp.maximum(row_max, jnp.max(masked, axis=-1))
        rescale = jnp.exp(row_max - new_max)
        weights = jnp.exp(masked - new_max[..., None])
        row_sum = row_sum * rescale + jnp.sum(weights, axis=-1)
        running = running * rescale[..., None] + jnp.einsum(
            "qhk,khd->qhd",
            weights.astype(jnp.bfloat16),
            key_block(value_rows, begin, block_size),
            preferred_element_type=jnp.float32,
        )
        return ((running, new_max, row_sum), None)

    start = (
        jnp.zeros((group, HEADS, HEAD_DIM), jnp.float32),
        jnp.zeros((group, HEADS), jnp.float32),
        jnp.zeros((group, HEADS), jnp.float32),
    )
    steps = jnp.arange(key_rows.shape[0] // block_size, dtype=jnp.int32)
    (running, row_max, row_sum), unused = lax.scan(forward_one_block, start, steps)
    safe_sum = jnp.where(query_seg[:, None] > 0, row_sum, 1.0)
    attended = (running / safe_sum[..., None]).reshape(group, HEADS * HEAD_DIM)
    return attended, (row_max, safe_sum)


def attention_backward(queries, key_rows, value_rows, query_seg, seg_row, attended, grad_mixed, kept):
    row_max, safe_sum = kept
    group, width = queries.shape
    seq_len = key_rows.shape[0]
    block_size = 512
    heads_in = queries.reshape(group, HEADS, HEAD_DIM)
    grads_in = grad_mixed.reshape(group, HEADS, HEAD_DIM)
    delta = jnp.sum(
        grads_in.astype(jnp.float32) * attended.reshape(group, HEADS, HEAD_DIM), axis=-1
    )

    def backward_one_block(state, block_index):
        grad_query, grad_keys, grad_values = state
        begin = block_index * block_size
        key_seg = lax.dynamic_slice_in_dim(seg_row, begin, block_size, 0)
        block_keys = key_block(key_rows, begin, block_size)
        block_values = key_block(value_rows, begin, block_size)
        masked = masked_scores(heads_in, block_keys, query_seg, key_seg)
        probs = jnp.exp(masked - row_max[..., None]) / safe_sum[..., None]
        grad_probs = jnp.einsum(
            "qhd,khd->qhk", grads_in, block_values, preferred_element_type=jnp.float32
        )
        grad_scores = (probs * (grad_probs - delta[..., None])).astype(jnp.bfloat16)
        grad_query = grad_query + jnp.einsum(
            "qhk,khd->qhd", grad_scores, block_keys, preferred_element_type=jnp.float32
        )
        key_part = jnp.einsum(
            "qhk,qhd->khd", grad_scores, heads_in, preferred_element_type=jnp.float32
        ).reshape(block_size, width)
        value_part = jnp.einsum(
            "qhk,qhd->khd", probs.astype(jnp.bfloat16), grads_in, preferred_element_type=jnp.float32
        ).reshape(block_size, width)
        grad_keys = lax.dynamic_update_slice_in_dim(
            grad_keys, key_part.astype(jnp.bfloat16), begin, 0
        )
        grad_values = lax.dynamic_update_slice_in_dim(
            grad_values, value_part.astype(jnp.bfloat16), begin, 0
        )
        return ((grad_query, grad_keys, grad_values), None)

    start = (
        jnp.zeros((group, HEADS, HEAD_DIM), jnp.float32),
        jnp.zeros((seq_len, width), jnp.bfloat16),
        jnp.zeros((seq_len, width), jnp.bfloat16),
    )
    steps = jnp.arange(seq_len // block_size, dtype=jnp.int32)
    (grad_query, grad_keys, grad_values), unused = lax.scan(backward_one_block, start, steps)
    grad_query = (grad_query.reshape(group, width) * 0.125).astype(jnp.bfloat16)
    return grad_query, grad_keys, grad_values


def shards(
    inputs,
    segments,
    qkv_weight,
    query_value_bias,
    output_weight,
    output_bias,
    attention_gain,
    attention_shift,
    up_weight,
    up_bias,
    down_weight,
    down_bias,
    final_gain,
    final_shift,
    cotangent,
):
    seq_count, group, width = inputs.shape
    seq_len = segments.shape[1]
    device_total = lax.axis_size("dp") * lax.axis_size("ctx")
    bits = index_bits()
    ctx_bits = axis_bits("ctx")
    first, second, third = exchange_orders()
    flat_in = inputs.reshape(group, width)
    seg_row = segments.reshape(seq_len)

    small = (
        query_value_bias,
        output_bias,
        attention_gain,
        attention_shift,
        up_bias,
        down_bias,
        final_gain,
        final_shift,
    )
    widths = [member.shape[0] for member in small]
    weight_rows = qkv_weight.shape[0]
    room = weight_rows * LANES
    packed = jnp.pad(jnp.concatenate(small), (0, room - sum(widths))).reshape(weight_rows, LANES)
    query_shard = jnp.concatenate([qkv_weight[:, :width], packed], axis=1)
    query_full = gather_rows(query_shard, third[::-1], bits)
    key_full = gather_rows(qkv_weight[:, width : 2 * width], second[::-1], bits)
    value_full = gather_rows(qkv_weight[:, 2 * width :], first[::-1], bits)
    seq_in = gather_rows(flat_in, ctx_bits[::-1], ctx_bits[::-1])
    out_full = gather_rows(output_weight, third[::-1], bits)
    up_full = gather_rows(up_weight, first[::-1], bits)
    down_full = gather_rows(down_weight, second[::-1], bits)
    query_weight = query_full[:, :width]
    spread = query_full[:, width:].reshape(device_total, room)
    members = []
    begin = 0
    for size in widths:
        members.append(spread[:, begin : begin + size].reshape(-1).astype(jnp.float32))
        begin += size
    bias_qv, bias_out, gain_one, shift_one, bias_up, bias_down, gain_two, shift_two = members

    offset = lax.axis_index("ctx") * group
    query_seg = lax.dynamic_slice_in_dim(seg_row, offset, group, 0)
    queries = (
        (jnp.dot(flat_in, query_weight, preferred_element_type=jnp.float32) + bias_qv[:width]) * 0.125
    ).astype(jnp.bfloat16)
    key_rows = jnp.dot(seq_in, key_full, preferred_element_type=jnp.float32).astype(jnp.bfloat16)
    value_rows = (
        jnp.dot(seq_in, value_full, preferred_element_type=jnp.float32) + bias_qv[width:]
    ).astype(jnp.bfloat16)
    attended, kept = attention_forward(queries, key_rows, value_rows, query_seg, seg_row)
    mixed_low = attended.astype(jnp.bfloat16)
    resid_one = (
        flat_in.astype(jnp.float32)
        + jnp.dot(mixed_low, out_full, preferred_element_type=jnp.float32)
        + bias_out
    )
    normed, first_back = jax.vjp(layer_norm, resid_one, gain_one, shift_one)
    normed_low = normed.astype(jnp.bfloat16)
    hidden_pre = jnp.dot(normed_low, up_full, preferred_element_type=jnp.float32) + bias_up
    hidden_low = exact_gelu(hidden_pre).astype(jnp.bfloat16)
    resid_two = (
        normed + jnp.dot(hidden_low, down_full, preferred_element_type=jnp.float32) + bias_down
    )
    result, final_back = jax.vjp(layer_norm, resid_two, gain_two, shift_two)
    output = result.astype(jnp.bfloat16).reshape(seq_count, group, width)

    grad_out = cotangent.reshape(group, width).astype(jnp.float32)
    grad_resid_two, final_gain_grad, final_shift_grad = final_back(grad_out)
    grad_down_in = grad_resid_two.astype(jnp.bfloat16)
    down_bias_grad = jnp.sum(grad_down_in.astype(jnp.float32), axis=0)
    down_weight_share = scatter_rows(inner_rows(hidden_low, grad_down_in), second, bits)
    grad_hidden = times_transpose(grad_down_in, down_full)
    unused_value, gelu_pull = jax.vjp(exact_gelu, hidden_pre)
    grad_pre = gelu_pull(grad_hidden)[0].astype(jnp.bfloat16)
    up_bias_grad = jnp.sum(grad_pre.astype(jnp.float32), axis=0)
    up_weight_share = scatter_rows(inner_rows(normed_low, grad_pre), first, bits)
    grad_normed = grad_resid_two + times_transpose(grad_pre, up_full)
    grad_resid_one, attention_gain_grad, attention_shift_grad = first_back(grad_normed)
    grad_mix_in = grad_resid_one.astype(jnp.bfloat16)
    output_bias_grad = jnp.sum(grad_mix_in.astype(jnp.float32), axis=0)
    output_weight_share = scatter_rows(inner_rows(mixed_low, grad_mix_in), third, bits)
    grad_mixed = times_transpose(grad_mix_in, out_full).astype(jnp.bfloat16)

    grad_query, grad_keys, grad_values = attention_backward(
        queries, key_rows, value_rows, query_seg, seg_row, attended, grad_mixed, kept
    )

    spread_back = times_transpose(grad_keys, key_full) + times_transpose(grad_values, value_full)
    own_back = scatter_rows(spread_back, ctx_bits, ctx_bits[::-1])
    query_sums = jnp.sum(grad_query.astype(jnp.float32), axis=0)
    value_sums = jnp.sum(grad_values.astype(jnp.float32), axis=0)
    qv_bias_grad = jnp.concatenate([query_sums, value_sums])
    small_grads = (
        qv_bias_grad,
        output_bias_grad,
        attention_gain_grad,
        attention_shift_grad,
        up_bias_grad,
        down_bias_grad,
        final_gain_grad,
        final_shift_grad,
    )
    packed_grads = jnp.concatenate(
        [member.reshape(device_total, size) for member, size in zip(small_grads, widths)], axis=1
    )
    packed_grads = jnp.pad(packed_grads, ((0, 0), (0, room - sum(widths))))
    packed_grads = packed_grads.reshape(device_total * weight_rows, LANES)
    key_share = scatter_rows(inner_rows(seq_in, grad_keys), second, bits)
    value_share = scatter_rows(inner_rows(seq_in, grad_values), first, bits)
    query_share = scatter_rows(
        jnp.concatenate([inner_rows(flat_in, grad_query), packed_grads], axis=1), third, bits
    )
    qkv_weight_share = jnp.concatenate([query_share[:, :width], key_share, value_share], axis=1)
    input_grad = (
        grad_resid_one + times_transpose(grad_query, query_weight) + own_back
    ).reshape(seq_count, group, width)
    flat_share = query_share[:, width:].reshape(room)
    pieces = []
    begin = 0
    for size in widths:
        pieces.append(flat_share[begin : begin + size])
        begin += size
    (
        qv_bias_share,
        output_bias_share,
        attention_gain_share,
        attention_shift_share,
        up_bias_share,
        down_bias_share,
        final_gain_share,
        final_shift_share,
    ) = pieces
    return (
        output,
        input_grad,
        qkv_weight_share,
        qv_bias_share,
        output_weight_share,
        output_bias_share,
        attention_gain_share,
        attention_shift_share,
        up_weight_share,
        up_bias_share,
        down_weight_share,
        down_bias_share,
        final_gain_share,
        final_shift_share,
    )


def solution(mesh):
    placed = (
        P("dp", "ctx", None),
        P("dp", None),
        P(("dp", "ctx"), None),
        P(("dp", "ctx")),
        P(("dp", "ctx"), None),
        P(("dp", "ctx")),
        P(("dp", "ctx")),
        P(("dp", "ctx")),
        P(("dp", "ctx"), None),
        P(("dp", "ctx")),
        P(("dp", "ctx"), None),
        P(("dp", "ctx")),
        P(("dp", "ctx")),
        P(("dp", "ctx")),
        P("dp", "ctx", None),
    )
    return jax.shard_map(
        shards,
        mesh=mesh,
        in_specs=placed,
        out_specs=(
            P("dp", "ctx", None),
            P("dp", "ctx", None),
            P(("dp", "ctx"), None),
            P(("dp", "ctx")),
            P(("dp", "ctx"), None),
            P(("dp", "ctx")),
            P(("dp", "ctx")),
            P(("dp", "ctx")),
            P(("dp", "ctx"), None),
            P(("dp", "ctx")),
            P(("dp", "ctx"), None),
            P(("dp", "ctx")),
            P(("dp", "ctx")),
            P(("dp", "ctx")),
        ),
        check_vma=False,
    )
```

```python
import jax
import jax.numpy as jnp
from jax import lax
from jax.experimental import pallas as pl
from jax.experimental.pallas import tpu as pltpu
from jax.sharding import PartitionSpec as P

HEADS = 12
HEAD_DIM = 64
LANES = 128

MASKED = -1000000000.0


def layer_norm(rows, gain, shift):
    center = jnp.mean(rows, axis=-1, keepdims=True)
    centred = rows - center
    spread = jnp.mean(centred * centred, axis=-1, keepdims=True)
    return centred * lax.rsqrt(spread + 1e-06) * gain + shift


def exact_gelu(values):
    return jax.nn.gelu(values, approximate=False)


def inner_rows(left, right):
    return lax.dot_general(
        left, right, (((0,), (0,)), ((), ())), preferred_element_type=jnp.float32
    )


def times_transpose(left, right):
    return lax.dot_general(
        left, right, (((1,), (1,)), ((), ())), preferred_element_type=jnp.float32
    )


def axis_bits(name):
    size = lax.axis_size(name)
    return [(name, 1 << k) for k in range(size.bit_length() - 1)]


def index_bits():
    return axis_bits("dp")[::-1] + axis_bits("ctx")[::-1]


def exchange_orders():
    dp, ctx = axis_bits("dp"), axis_bits("ctx")
    core, side, near, far = ctx[:1], ctx[1:], dp[:1], dp[1:]
    return (
        core + near + side + far,
        core + side + near + far,
        core + far[:1] + near + side + far[1:],
    )


def partner(value, bit):
    name, step = bit
    pairs = [(i, i ^ step) for i in range(lax.axis_size(name))]
    return lax.ppermute(value, name, pairs)


def own_bit(bit):
    name, step = bit
    return (lax.axis_index(name) // step) % 2


def gather_rows(shard, order, bits):
    rows, cols = shard.shape
    have = []
    held = shard
    for bit in order:
        theirs = partner(held, bit)
        place = sum(1 for other in have if bits.index(other) < bits.index(bit))
        shape = [1] * (held.ndim + 1)
        shape[place] = 2
        mine = jnp.arange(2).reshape(shape) == own_bit(bit)
        held = jnp.where(mine, jnp.expand_dims(held, place), jnp.expand_dims(theirs, place))
        have.append(bit)
    return held.reshape(rows << len(order), cols)


def scatter_rows(full, order, bits):
    rows, cols = full.shape
    have = list(bits)
    held = full.astype(jnp.bfloat16).reshape([2] * len(bits) + [rows >> len(bits), cols])
    for bit in order:
        place = have.index(bit)
        mine = own_bit(bit)
        keep = lax.dynamic_index_in_dim(held, mine, place, keepdims=False)
        send = lax.dynamic_index_in_dim(held, 1 - mine, place, keepdims=False)
        total = keep.astype(jnp.float32) + partner(send, bit).astype(jnp.float32)
        have.remove(bit)
        held = total.astype(jnp.bfloat16) if have else total
    return held


PAIR = 2 * HEAD_DIM
QUERY_TILE = 256
KEY_TILE = 256


def forward_kernel(low_ref, high_ref, q_ref, k_ref, v_ref, qseg_ref, kseg_ref, o_ref, lse_ref):
    lane = lax.broadcasted_iota(jnp.int32, (1, PAIR), 1)
    left = lane < HEAD_DIM
    for tile in range(q_ref.shape[0] // QUERY_TILE):
        rows = pl.ds(tile * QUERY_TILE, QUERY_TILE)
        q = q_ref[rows, :]
        qseg = qseg_ref[rows, :]
        parts = [jnp.where(left, q, jnp.zeros_like(q)), jnp.where(left, jnp.zeros_like(q), q)]

        def step(block, state):
            keys = pl.ds(pl.multiple_of(block * KEY_TILE, KEY_TILE), KEY_TILE)
            k = k_ref[keys, :]
            v = v_ref[keys, :]
            allowed = qseg == kseg_ref[block]
            out = []
            for part, (top, total, held) in zip(parts, state):
                s = lax.dot_general(
                    part, k, (((1,), (1,)), ((), ())), preferred_element_type=jnp.float32
                )
                s = jnp.where(allowed, s, MASKED)
                new_top = jnp.maximum(top, jnp.max(s, axis=1, keepdims=True))
                p = jnp.exp(s - new_top)
                scale = jnp.exp(top - new_top)
                total = total * scale + jnp.sum(p, axis=1, keepdims=True)
                held = held * scale + jnp.dot(
                    p.astype(jnp.bfloat16), v, preferred_element_type=jnp.float32
                )
                out.append((new_top, total, held))
            return tuple(out)

        column = jnp.zeros((QUERY_TILE, 1), jnp.float32)
        start = (column, column, jnp.zeros((QUERY_TILE, PAIR), jnp.float32))
        state = lax.fori_loop(low_ref[tile], high_ref[tile], step, (start, start))
        outs, logs = [], []
        for top, total, held in state:
            safe = jnp.where(qseg > 0, total, 1.0)
            outs.append(held / safe)
            logs.append(top + jnp.log(safe))
        o_ref[rows, :] = jnp.where(left, outs[0], outs[1])
        lse_ref[rows, :] = jnp.where(left, logs[0], logs[1])


def backward_kernel(
    low_ref, high_ref, q_ref, k_ref, v_ref, qseg_ref, kseg_ref, o_ref, lse_ref, do_ref,
    dq_ref, dk_ref, dv_ref, dk_sum, dv_sum,
):
    lane = lax.broadcasted_iota(jnp.int32, (1, PAIR), 1)
    left = lane < HEAD_DIM
    dk_sum[...] = jnp.zeros_like(dk_sum)
    dv_sum[...] = jnp.zeros_like(dv_sum)
    for tile in range(q_ref.shape[0] // QUERY_TILE):
        rows = pl.ds(tile * QUERY_TILE, QUERY_TILE)
        q = q_ref[rows, :]
        do = do_ref[rows, :]
        qseg = qseg_ref[tile]
        none = jnp.zeros_like(q)
        q_parts = [jnp.where(left, q, none), jnp.where(left, none, q)]
        do_parts = [jnp.where(left, do, none), jnp.where(left, none, do)]
        lse_t = lse_ref[rows, :].T
        logs = [lse_t[:1, :], lse_t[HEAD_DIM : HEAD_DIM + 1, :]]
        prod_t = (do.astype(jnp.float32) * o_ref[rows, :]).T
        deltas = [
            jnp.sum(prod_t[:HEAD_DIM, :], axis=0, keepdims=True),
            jnp.sum(prod_t[HEAD_DIM:, :], axis=0, keepdims=True),
        ]

        def step(block, dq):
            keys = pl.ds(pl.multiple_of(block * KEY_TILE, KEY_TILE), KEY_TILE)
            k = k_ref[keys, :]
            v = v_ref[keys, :]
            allowed = kseg_ref[keys, :] == qseg
            dk, dv, dqs = [], [], []
            for q_part, do_part, log, delta in zip(q_parts, do_parts, logs, deltas):
                s = lax.dot_general(
                    k, q_part, (((1,), (1,)), ((), ())), preferred_element_type=jnp.float32
                )
                p = jnp.exp(jnp.where(allowed, s, MASKED) - log)
                dp = lax.dot_general(
                    v, do_part, (((1,), (1,)), ((), ())), preferred_element_type=jnp.float32
                )
                ds = (p * (dp - delta)).astype(jnp.bfloat16)
                dv.append(jnp.dot(p.astype(jnp.bfloat16), do_part, preferred_element_type=jnp.float32))
                dk.append(jnp.dot(ds, q_part, preferred_element_type=jnp.float32))
                dqs.append(
                    lax.dot_general(
                        ds, k, (((0,), (0,)), ((), ())), preferred_element_type=jnp.float32
                    )
                )
            dk_sum[keys, :] += dk[0] + dk[1]
            dv_sum[keys, :] += dv[0] + dv[1]
            return dq + jnp.where(left, dqs[0], dqs[1])

        start = jnp.zeros((QUERY_TILE, PAIR), jnp.float32)
        dq = lax.fori_loop(low_ref[tile], high_ref[tile], step, start)
        dq_ref[rows, :] = (dq * 0.125).astype(jnp.bfloat16)
    dk_ref[...] = dk_sum[...].astype(jnp.bfloat16)
    dv_ref[...] = dv_sum[...].astype(jnp.bfloat16)


def key_ranges(query_seg, seg_row):
    tiles = query_seg.reshape(-1, QUERY_TILE)
    first = tiles[:, 0]
    last = jnp.max(tiles, axis=1)
    real = seg_row > 0
    before = jnp.sum((real & (seg_row < first[:, None])).astype(jnp.int32), axis=1)
    until = jnp.sum((real & (seg_row <= last[:, None])).astype(jnp.int32), axis=1)
    low = before // KEY_TILE
    high = (until + KEY_TILE - 1) // KEY_TILE
    return jnp.where(first > 0, low, 0), jnp.where(first > 0, high, 0)


def column_block(rows):
    return pl.BlockSpec((rows, PAIR), lambda pair, low, high: (0, pair))


def whole_block(shape):
    return pl.BlockSpec(shape, lambda pair, low, high: (0,) * len(shape))


def attention_forward(queries, key_rows, value_rows, query_seg, seg_row):
    group, width = queries.shape
    seq_len = key_rows.shape[0]
    low, high = key_ranges(query_seg, seg_row)
    query_ids = jnp.where(query_seg > 0, query_seg, -1)
    return pl.pallas_call(
        forward_kernel,
        grid_spec=pltpu.PrefetchScalarGridSpec(
            num_scalar_prefetch=2,
            grid=(width // PAIR,),
            in_specs=[
                column_block(group),
                column_block(seq_len),
                column_block(seq_len),
                whole_block((group, 1)),
                whole_block((seq_len // KEY_TILE, 1, KEY_TILE)),
            ],
            out_specs=[column_block(group), column_block(group)],
        ),
        out_shape=[jax.ShapeDtypeStruct((group, width), jnp.float32)] * 2,
        compiler_params=pltpu.CompilerParams(vmem_limit_bytes=48 << 20),
        cost_estimate=pl.CostEstimate(
            flops=4 * group * seq_len * width,
            bytes_accessed=4 * seq_len * width + 10 * group * width,
            transcendentals=group * seq_len * (width // HEAD_DIM),
        ),
        name="attention_forward",
    )(low, high, queries, key_rows, value_rows, query_ids[:, None], seg_row.reshape(-1, 1, KEY_TILE))


def attention_backward(queries, key_rows, value_rows, query_seg, seg_row, attended, grad_mixed, kept):
    group, width = queries.shape
    seq_len = key_rows.shape[0]
    low, high = key_ranges(query_seg, seg_row)
    query_ids = jnp.where(query_seg > 0, query_seg, -1)
    return pl.pallas_call(
        backward_kernel,
        grid_spec=pltpu.PrefetchScalarGridSpec(
            num_scalar_prefetch=2,
            grid=(width // PAIR,),
            in_specs=[
                column_block(group),
                column_block(seq_len),
                column_block(seq_len),
                whole_block((group // QUERY_TILE, 1, QUERY_TILE)),
                whole_block((seq_len, 1)),
                column_block(group),
                column_block(group),
                column_block(group),
            ],
            out_specs=[column_block(group), column_block(seq_len), column_block(seq_len)],
            scratch_shapes=[pltpu.VMEM((seq_len, PAIR), jnp.float32)] * 2,
        ),
        out_shape=[
            jax.ShapeDtypeStruct((group, width), jnp.bfloat16),
            jax.ShapeDtypeStruct((seq_len, width), jnp.bfloat16),
            jax.ShapeDtypeStruct((seq_len, width), jnp.bfloat16),
        ],
        compiler_params=pltpu.CompilerParams(vmem_limit_bytes=48 << 20),
        cost_estimate=pl.CostEstimate(
            flops=10 * group * seq_len * width,
            bytes_accessed=8 * seq_len * width + 14 * group * width,
            transcendentals=group * seq_len * (width // HEAD_DIM),
        ),
        name="attention_backward",
    )(
        low, high, queries, key_rows, value_rows,
        query_ids.reshape(-1, 1, QUERY_TILE), seg_row[:, None], attended, kept, grad_mixed,
    )


def shards(
    inputs,
    segments,
    qkv_weight,
    query_value_bias,
    output_weight,
    output_bias,
    attention_gain,
    attention_shift,
    up_weight,
    up_bias,
    down_weight,
    down_bias,
    final_gain,
    final_shift,
    cotangent,
):
    seq_count, group, width = inputs.shape
    seq_len = segments.shape[1]
    device_total = lax.axis_size("dp") * lax.axis_size("ctx")
    bits = index_bits()
    ctx_bits = axis_bits("ctx")
    first, second, third = exchange_orders()
    flat_in = inputs.reshape(group, width)
    seg_row = segments.reshape(seq_len)

    small = (
        query_value_bias,
        output_bias,
        attention_gain,
        attention_shift,
        up_bias,
        down_bias,
        final_gain,
        final_shift,
    )
    widths = [member.shape[0] for member in small]
    weight_rows = qkv_weight.shape[0]
    room = weight_rows * LANES
    packed = jnp.pad(jnp.concatenate(small), (0, room - sum(widths))).reshape(weight_rows, LANES)
    query_shard = jnp.concatenate([qkv_weight[:, :width], packed], axis=1)
    query_full = gather_rows(query_shard, third[::-1], bits)
    key_full = gather_rows(qkv_weight[:, width : 2 * width], second[::-1], bits)
    value_full = gather_rows(qkv_weight[:, 2 * width :], first[::-1], bits)
    seq_in = gather_rows(flat_in, ctx_bits[::-1], ctx_bits[::-1])
    out_full = gather_rows(output_weight, third[::-1], bits)
    up_full = gather_rows(up_weight, first[::-1], bits)
    down_full = gather_rows(down_weight, second[::-1], bits)
    query_weight = query_full[:, :width]
    spread = query_full[:, width:].reshape(device_total, room)
    members = []
    begin = 0
    for size in widths:
        members.append(spread[:, begin : begin + size].reshape(-1).astype(jnp.float32))
        begin += size
    bias_qv, bias_out, gain_one, shift_one, bias_up, bias_down, gain_two, shift_two = members

    offset = lax.axis_index("ctx") * group
    query_seg = lax.dynamic_slice_in_dim(seg_row, offset, group, 0)
    queries = (
        (jnp.dot(flat_in, query_weight, preferred_element_type=jnp.float32) + bias_qv[:width]) * 0.125
    ).astype(jnp.bfloat16)
    key_rows = jnp.dot(seq_in, key_full, preferred_element_type=jnp.float32).astype(jnp.bfloat16)
    value_rows = (
        jnp.dot(seq_in, value_full, preferred_element_type=jnp.float32) + bias_qv[width:]
    ).astype(jnp.bfloat16)
    attended, kept = attention_forward(queries, key_rows, value_rows, query_seg, seg_row)
    mixed_low = attended.astype(jnp.bfloat16)
    resid_one = (
        flat_in.astype(jnp.float32)
        + jnp.dot(mixed_low, out_full, preferred_element_type=jnp.float32)
        + bias_out
    )
    normed, first_back = jax.vjp(layer_norm, resid_one, gain_one, shift_one)
    normed_low = normed.astype(jnp.bfloat16)
    hidden_pre = jnp.dot(normed_low, up_full, preferred_element_type=jnp.float32) + bias_up
    hidden_low = exact_gelu(hidden_pre).astype(jnp.bfloat16)
    resid_two = (
        normed + jnp.dot(hidden_low, down_full, preferred_element_type=jnp.float32) + bias_down
    )
    result, final_back = jax.vjp(layer_norm, resid_two, gain_two, shift_two)
    output = result.astype(jnp.bfloat16).reshape(seq_count, group, width)

    grad_out = cotangent.reshape(group, width).astype(jnp.float32)
    grad_resid_two, final_gain_grad, final_shift_grad = final_back(grad_out)
    grad_down_in = grad_resid_two.astype(jnp.bfloat16)
    down_bias_grad = jnp.sum(grad_down_in.astype(jnp.float32), axis=0)
    down_weight_share = scatter_rows(inner_rows(hidden_low, grad_down_in), second, bits)
    grad_hidden = times_transpose(grad_down_in, down_full)
    unused_value, gelu_pull = jax.vjp(exact_gelu, hidden_pre)
    grad_pre = gelu_pull(grad_hidden)[0].astype(jnp.bfloat16)
    up_bias_grad = jnp.sum(grad_pre.astype(jnp.float32), axis=0)
    up_weight_share = scatter_rows(inner_rows(normed_low, grad_pre), first, bits)
    grad_normed = grad_resid_two + times_transpose(grad_pre, up_full)
    grad_resid_one, attention_gain_grad, attention_shift_grad = first_back(grad_normed)
    grad_mix_in = grad_resid_one.astype(jnp.bfloat16)
    output_bias_grad = jnp.sum(grad_mix_in.astype(jnp.float32), axis=0)
    output_weight_share = scatter_rows(inner_rows(mixed_low, grad_mix_in), third, bits)
    grad_mixed = times_transpose(grad_mix_in, out_full).astype(jnp.bfloat16)

    grad_query, grad_keys, grad_values = attention_backward(
        queries, key_rows, value_rows, query_seg, seg_row, attended, grad_mixed, kept
    )

    spread_back = times_transpose(grad_keys, key_full) + times_transpose(grad_values, value_full)
    own_back = scatter_rows(spread_back, ctx_bits, ctx_bits[::-1])
    query_sums = jnp.sum(grad_query.astype(jnp.float32), axis=0)
    value_sums = jnp.sum(grad_values.astype(jnp.float32), axis=0)
    qv_bias_grad = jnp.concatenate([query_sums, value_sums])
    small_grads = (
        qv_bias_grad,
        output_bias_grad,
        attention_gain_grad,
        attention_shift_grad,
        up_bias_grad,
        down_bias_grad,
        final_gain_grad,
        final_shift_grad,
    )
    packed_grads = jnp.concatenate(
        [member.reshape(device_total, size) for member, size in zip(small_grads, widths)], axis=1
    )
    packed_grads = jnp.pad(packed_grads, ((0, 0), (0, room - sum(widths))))
    packed_grads = packed_grads.reshape(device_total * weight_rows, LANES)
    key_share = scatter_rows(inner_rows(seq_in, grad_keys), second, bits)
    value_share = scatter_rows(inner_rows(seq_in, grad_values), first, bits)
    query_share = scatter_rows(
        jnp.concatenate([inner_rows(flat_in, grad_query), packed_grads], axis=1), third, bits
    )
    qkv_weight_share = jnp.concatenate([query_share[:, :width], key_share, value_share], axis=1)
    input_grad = (
        grad_resid_one + times_transpose(grad_query, query_weight) + own_back
    ).reshape(seq_count, group, width)
    flat_share = query_share[:, width:].reshape(room)
    pieces = []
    begin = 0
    for size in widths:
        pieces.append(flat_share[begin : begin + size])
        begin += size
    (
        qv_bias_share,
        output_bias_share,
        attention_gain_share,
        attention_shift_share,
        up_bias_share,
        down_bias_share,
        final_gain_share,
        final_shift_share,
    ) = pieces
    return (
        output,
        input_grad,
        qkv_weight_share,
        qv_bias_share,
        output_weight_share,
        output_bias_share,
        attention_gain_share,
        attention_shift_share,
        up_weight_share,
        up_bias_share,
        down_weight_share,
        down_bias_share,
        final_gain_share,
        final_shift_share,
    )


def solution(mesh):
    placed = (
        P("dp", "ctx", None),
        P("dp", None),
        P(("dp", "ctx"), None),
        P(("dp", "ctx")),
        P(("dp", "ctx"), None),
        P(("dp", "ctx")),
        P(("dp", "ctx")),
        P(("dp", "ctx")),
        P(("dp", "ctx"), None),
        P(("dp", "ctx")),
        P(("dp", "ctx"), None),
        P(("dp", "ctx")),
        P(("dp", "ctx")),
        P(("dp", "ctx")),
        P("dp", "ctx", None),
    )
    return jax.shard_map(
        shards,
        mesh=mesh,
        in_specs=placed,
        out_specs=(
            P("dp", "ctx", None),
            P("dp", "ctx", None),
            P(("dp", "ctx"), None),
            P(("dp", "ctx")),
            P(("dp", "ctx"), None),
            P(("dp", "ctx")),
            P(("dp", "ctx")),
            P(("dp", "ctx")),
            P(("dp", "ctx"), None),
            P(("dp", "ctx")),
            P(("dp", "ctx"), None),
            P(("dp", "ctx")),
            P(("dp", "ctx")),
            P(("dp", "ctx")),
        ),
        check_vma=False,
    )
```

```python
import jax
import jax.numpy as jnp
from jax import lax
from jax.experimental import pallas as pl
from jax.experimental.pallas import tpu as pltpu
from jax.sharding import PartitionSpec as P

HEADS = 12
HEAD_DIM = 64
LANES = 128

MASKED = -1000000000.0


def layer_norm(rows, gain, shift):
    center = jnp.mean(rows, axis=-1, keepdims=True)
    centred = rows - center
    spread = jnp.mean(centred * centred, axis=-1, keepdims=True)
    return centred * lax.rsqrt(spread + 1e-06) * gain + shift


def gelu_parts(values):
    below = 0.5 * (1.0 + lax.erf(values * 0.7071067811865476))
    density = 0.3989422804014327 * jnp.exp(-0.5 * values * values)
    return values * below, below + values * density


def inner_rows(left, right):
    return lax.dot_general(
        left, right, (((0,), (0,)), ((), ())), preferred_element_type=jnp.float32
    )


def times_transpose(left, right):
    return lax.dot_general(
        left, right, (((1,), (1,)), ((), ())), preferred_element_type=jnp.float32
    )


def axis_bits(name):
    size = lax.axis_size(name)
    return [(name, 1 << k) for k in range(size.bit_length() - 1)]


def index_bits():
    return axis_bits("dp")[::-1] + axis_bits("ctx")[::-1]


def exchange_orders():
    dp, ctx = axis_bits("dp"), axis_bits("ctx")
    core, side, near, far = ctx[:1], ctx[1:], dp[:1], dp[1:]
    return (
        core + near + side + far,
        core + side + near + far,
        core + far[:1] + near + side + far[1:],
    )


def partner(value, bit):
    name, step = bit
    pairs = [(i, i ^ step) for i in range(lax.axis_size(name))]
    return lax.ppermute(value, name, pairs)


def own_bit(bit):
    name, step = bit
    return (lax.axis_index(name) // step) % 2


PAIR = 2 * HEAD_DIM
CHUNK = 2 * PAIR
QUERY_TILE = 256
KEY_TILE = 256


def head_parts(ref, rows):
    lane = lax.broadcasted_iota(jnp.int32, (1, PAIR), 1)
    parts = []
    for begin in range(0, CHUNK, PAIR):
        both = ref[rows, begin : begin + PAIR]
        none = jnp.zeros_like(both)
        parts.append(jnp.where(lane < HEAD_DIM, both, none))
        parts.append(jnp.where(lane < HEAD_DIM, none, both))
    return parts


def forward_kernel(low_ref, high_ref, q_ref, kv_ref, qseg_ref, kseg_ref, o_ref, lse_ref):
    for tile in range(q_ref.shape[0] // QUERY_TILE):
        rows = pl.ds(tile * QUERY_TILE, QUERY_TILE)
        qseg = qseg_ref[tile]
        parts = head_parts(q_ref, rows)

        def step(block, state):
            keys = pl.ds(pl.multiple_of(block * KEY_TILE, KEY_TILE), KEY_TILE)
            allowed = kseg_ref[keys, :] == qseg
            out = []
            for pair in range(CHUNK // PAIR):
                begin = pair * PAIR
                k = kv_ref[keys, begin : begin + PAIR]
                v_t = kv_ref[keys, CHUNK + begin : CHUNK + begin + PAIR].T
                for side in range(2):
                    head = 2 * pair + side
                    top, total, held = state[head]
                    s = lax.dot_general(
                        k, parts[head], (((1,), (1,)), ((), ())), preferred_element_type=jnp.float32
                    )
                    s = jnp.where(allowed, s, MASKED)
                    new_top = jnp.maximum(top, jnp.max(s, axis=0, keepdims=True))
                    p = jnp.exp(s - new_top)
                    scale = jnp.exp(top - new_top)
                    total = total * scale + jnp.sum(p, axis=0, keepdims=True)
                    held = held * scale + jnp.dot(
                        v_t[side * HEAD_DIM : (side + 1) * HEAD_DIM, :],
                        p.astype(jnp.bfloat16),
                        preferred_element_type=jnp.float32,
                    )
                    out.append((new_top, total, held))
            return tuple(out)

        row = jnp.zeros((1, QUERY_TILE), jnp.float32)
        start = (row, row, jnp.zeros((HEAD_DIM, QUERY_TILE), jnp.float32))
        state = lax.fori_loop(low_ref[tile], high_ref[tile], step, (start,) * (CHUNK // HEAD_DIM))
        outs = []
        for head, (top, total, held) in enumerate(state):
            safe = jnp.where(qseg > 0, total, 1.0)
            outs.append(held / safe)
            lse_ref[head : head + 1, rows] = top + jnp.log(safe)
        for pair in range(CHUNK // PAIR):
            both = jnp.concatenate(outs[2 * pair : 2 * pair + 2], axis=0)
            o_ref[rows, pair * PAIR : (pair + 1) * PAIR] = both.T


def backward_kernel(
    low_ref, high_ref, q_ref, kv_ref, qseg_ref, kseg_ref, o_ref, lse_ref, do_ref,
    dq_ref, dkv_ref, sums,
):
    sums[...] = jnp.zeros_like(sums)
    for tile in range(q_ref.shape[0] // QUERY_TILE):
        rows = pl.ds(tile * QUERY_TILE, QUERY_TILE)
        qseg = qseg_ref[tile]
        q_parts = head_parts(q_ref, rows)
        do_parts = head_parts(do_ref, rows)
        deltas = []
        for begin in range(0, CHUNK, PAIR):
            do = do_ref[rows, begin : begin + PAIR].astype(jnp.float32)
            prod_t = (do * o_ref[rows, begin : begin + PAIR]).T
            deltas.append(jnp.sum(prod_t[:HEAD_DIM, :], axis=0, keepdims=True))
            deltas.append(jnp.sum(prod_t[HEAD_DIM:, :], axis=0, keepdims=True))
        logs = [lse_ref[head : head + 1, rows] for head in range(CHUNK // HEAD_DIM)]

        def step(block, state):
            keys = pl.ds(pl.multiple_of(block * KEY_TILE, KEY_TILE), KEY_TILE)
            allowed = kseg_ref[keys, :] == qseg
            out = []
            for pair in range(CHUNK // PAIR):
                begin = pair * PAIR
                k = kv_ref[keys, begin : begin + PAIR]
                v = kv_ref[keys, CHUNK + begin : CHUNK + begin + PAIR]
                k_t = k.T
                dk, dv = 0.0, 0.0
                for side in range(2):
                    head = 2 * pair + side
                    s = lax.dot_general(
                        k, q_parts[head], (((1,), (1,)), ((), ())), preferred_element_type=jnp.float32
                    )
                    p = jnp.exp(jnp.where(allowed, s, MASKED) - logs[head])
                    dp = lax.dot_general(
                        v, do_parts[head], (((1,), (1,)), ((), ())), preferred_element_type=jnp.float32
                    )
                    ds = (p * (dp - deltas[head])).astype(jnp.bfloat16)
                    dv += jnp.dot(
                        p.astype(jnp.bfloat16), do_parts[head], preferred_element_type=jnp.float32
                    )
                    dk += jnp.dot(ds, q_parts[head], preferred_element_type=jnp.float32)
                    out.append(
                        state[head]
                        + jnp.dot(
                            k_t[side * HEAD_DIM : (side + 1) * HEAD_DIM, :],
                            ds,
                            preferred_element_type=jnp.float32,
                        )
                    )
                sums[keys, begin : begin + PAIR] += dk
                sums[keys, CHUNK + begin : CHUNK + begin + PAIR] += dv
            return tuple(out)

        start = jnp.zeros((HEAD_DIM, QUERY_TILE), jnp.float32)
        state = lax.fori_loop(low_ref[tile], high_ref[tile], step, (start,) * (CHUNK // HEAD_DIM))
        for pair in range(CHUNK // PAIR):
            both = jnp.concatenate(state[2 * pair : 2 * pair + 2], axis=0)
            dq_ref[rows, pair * PAIR : (pair + 1) * PAIR] = (both.T * 0.125).astype(jnp.bfloat16)
    dkv_ref[...] = sums[...].astype(jnp.bfloat16)


def key_ranges(query_seg, seg_row):
    tiles = query_seg.reshape(-1, QUERY_TILE)
    first = tiles[:, 0]
    last = jnp.max(tiles, axis=1)
    real = seg_row > 0
    before = jnp.sum((real & (seg_row < first[:, None])).astype(jnp.int32), axis=1)
    until = jnp.sum((real & (seg_row <= last[:, None])).astype(jnp.int32), axis=1)
    low = before // KEY_TILE
    high = (until + KEY_TILE - 1) // KEY_TILE
    return jnp.where(first > 0, low, 0), jnp.where(first > 0, high, 0)


def whole_block(shape):
    return pl.BlockSpec(shape, lambda step, low, high: (0,) * len(shape))


def attention_call(kernel, name, where, operands, out_shape, scratch, matmuls):
    group = operands[0].shape[0]
    low, high, query_ids, key_ids = where
    queries, pairs = operands[:2]
    operands = [queries, pairs, query_ids, key_ids, *operands[2:]]
    return pl.pallas_call(
        kernel,
        grid_spec=pltpu.PrefetchScalarGridSpec(
            num_scalar_prefetch=2,
            grid=(1,),
            in_specs=[whole_block(operand.shape) for operand in operands],
            out_specs=[whole_block(member.shape) for member in out_shape],
            scratch_shapes=scratch,
        ),
        out_shape=out_shape,
        compiler_params=pltpu.CompilerParams(vmem_limit_bytes=40 << 20),
        cost_estimate=pl.CostEstimate(
            flops=matmuls * group * CHUNK, bytes_accessed=group * CHUNK, transcendentals=0
        ),
        name=name,
    )(low, high, *operands)


def attention_forward(where, queries, pairs):
    group = queries.shape[0]
    out_shape = [
        jax.ShapeDtypeStruct((group, CHUNK), jnp.float32),
        jax.ShapeDtypeStruct((CHUNK // HEAD_DIM, group), jnp.float32),
    ]
    return attention_call(
        forward_kernel, "attention_forward", where, [queries, pairs], out_shape, [], 2
    )


def attention_backward(where, queries, pairs, attended, logs, grad_mixed):
    group, seq_len = queries.shape[0], pairs.shape[0]
    out_shape = [
        jax.ShapeDtypeStruct((group, CHUNK), jnp.bfloat16),
        jax.ShapeDtypeStruct((seq_len, 2 * CHUNK), jnp.bfloat16),
    ]
    return attention_call(
        backward_kernel,
        "attention_backward",
        where,
        [queries, pairs, attended, logs, grad_mixed],
        out_shape,
        [pltpu.VMEM((seq_len, 2 * CHUNK), jnp.float32)],
        5,
    )


class Exchange:
    def __init__(self, held, order, bits):
        self.held, self.todo, self.bits = held, list(order), bits
        self.flying = None

    def finish(self, *after):
        if self.flying is None:
            return
        bit, keep, theirs = self.flying
        self.flying = None
        if after:
            theirs = lax.optimization_barrier((theirs, *after))[0]
        self.merge(bit, keep, theirs)

    def advance(self, *after):
        self.finish(*after)
        if self.todo:
            bit = self.todo.pop(0)
            keep, send = self.split(bit)
            self.flying = bit, keep, partner(send, bit)

    def run(self, steps=None):
        for step in range(len(self.todo) if steps is None else steps):
            self.advance()
            self.finish()
        return self


class Gather(Exchange):
    def __init__(self, shard, order, bits):
        super().__init__(shard, order, bits)
        self.rows, self.cols = shard.shape
        self.have = []

    def split(self, bit):
        return self.held, self.held

    def merge(self, bit, keep, theirs):
        place = sum(1 for other in self.have if self.bits.index(other) < self.bits.index(bit))
        shape = [1] * (keep.ndim + 1)
        shape[place] = 2
        mine = jnp.arange(2).reshape(shape) == own_bit(bit)
        self.held = jnp.where(mine, jnp.expand_dims(keep, place), jnp.expand_dims(theirs, place))
        self.have.append(bit)

    def full(self):
        return self.held.reshape(self.rows << len(self.have), self.cols)


class Scatter(Exchange):
    def __init__(self, full, order, bits):
        rows, cols = full.shape
        shape = [2] * len(bits) + [rows >> len(bits), cols]
        super().__init__(full.astype(jnp.bfloat16).reshape(shape), order, bits)
        self.have = list(bits)

    def split(self, bit):
        place = self.have.index(bit)
        mine = own_bit(bit)
        keep = lax.dynamic_index_in_dim(self.held, mine, place, keepdims=False)
        send = lax.dynamic_index_in_dim(self.held, 1 - mine, place, keepdims=False)
        return keep, send

    def merge(self, bit, keep, theirs):
        total = keep.astype(jnp.float32) + theirs.astype(jnp.float32)
        self.have.remove(bit)
        self.held = total.astype(jnp.bfloat16) if self.have else total


def spots(count, rows):
    places = [(k % rows, k // rows * LANES) for k in range(count)]
    return places, (count + rows - 1) // rows * LANES


def pack(members, rows):
    places, columns = spots(len(members), rows)
    total = 0
    for member, (row, column) in zip(members, places):
        count, size = member.shape
        edges = ((0, 0), (row, rows - 1 - row), (column, columns - column - size))
        total = total + jnp.pad(member[:, None, :], edges)
    return total.reshape(-1, columns)


def unpack(packed, widths, rows):
    places, columns = spots(len(widths), rows)
    blocks = packed.reshape(-1, rows, columns)
    return [
        blocks[:, row, column : column + size]
        for (row, column), size in zip(places, widths)
    ]


def hold(value, *exchanges):
    held = lax.optimization_barrier((value, *[member.held for member in exchanges]))
    for member, new in zip(exchanges, held[1:]):
        member.held = new
    return held[0]


def step_beside(value, *exchanges, after=()):
    for member in exchanges:
        member.finish(*after)
    value = hold(value, *exchanges)
    for member in exchanges:
        member.advance()
    return value


def shards(
    inputs,
    segments,
    qkv_weight,
    query_value_bias,
    output_weight,
    output_bias,
    attention_gain,
    attention_shift,
    up_weight,
    up_bias,
    down_weight,
    down_bias,
    final_gain,
    final_shift,
    cotangent,
):
    seq_count, group, width = inputs.shape
    seq_len = segments.shape[1]
    device_total = lax.axis_size("dp") * lax.axis_size("ctx")
    bits = index_bits()
    ctx_bits = axis_bits("ctx")
    first, second, third = orders = exchange_orders()
    flat_in = inputs.reshape(group, width)
    seg_row = segments.reshape(seq_len)
    chunks = range(width // CHUNK)

    small = (
        query_value_bias,
        output_bias,
        attention_gain,
        attention_shift,
        up_bias,
        down_bias,
        final_gain,
        final_shift,
    )
    widths = [member.shape[0] for member in small]
    weight_rows = qkv_weight.shape[0]
    packed = pack([member[None, :] for member in small], weight_rows)

    blocks = down_weight.shape[0] // weight_rows
    shards_beside = [up_weight, output_weight]
    for block in range(blocks):
        shards_beside.append(down_weight[block * weight_rows : (block + 1) * weight_rows])
    later = lax.all_gather(
        jnp.concatenate(shards_beside, axis=1), ("dp", "ctx"), axis=0, tiled=True
    )
    hidden = up_weight.shape[1]

    seq_gather = Gather(flat_in, ctx_bits[::-1], ctx_bits[::-1])
    gathers = []
    for chunk in chunks:
        parts = [
            qkv_weight[:, base + chunk * CHUNK : base + (chunk + 1) * CHUNK]
            for base in (0, width, 2 * width)
        ]
        if chunk == 0:
            parts.append(packed)
        gathers.append(Gather(jnp.concatenate(parts, axis=1), orders[2 - chunk % 3][::-1], bits))
    seq_gather.run(len(ctx_bits) - 2)
    seq_gather.advance()
    for member in gathers:
        member.run(len(bits) - 2)
    seq_gather.advance(*[member.held for member in gathers])
    for member in gathers:
        member.run()
    seq_gather.finish()
    seq_in = seq_gather.full()
    weights = [member.full() for member in gathers]
    members = unpack(weights[0][:, 3 * CHUNK :], widths, weight_rows)
    members = [member.reshape(-1).astype(jnp.float32) for member in members]
    bias_qv, bias_out, gain_one, shift_one, bias_up, bias_down, gain_two, shift_two = members

    offset = lax.axis_index("ctx") * group
    query_seg = lax.dynamic_slice_in_dim(seg_row, offset, group, 0)
    query_ids = jnp.where(query_seg > 0, query_seg, -1).reshape(-1, 1, QUERY_TILE)
    where = (*key_ranges(query_seg, seg_row), query_ids, seg_row[:, None])

    queries, pairs, attended, logs = [], [], [], []
    for chunk in chunks:
        begin = chunk * CHUNK
        weight = weights[chunk]
        query_bias = bias_qv[begin : begin + CHUNK]
        value_bias = bias_qv[width + begin : width + begin + CHUNK]
        pair_bias = jnp.concatenate([jnp.zeros_like(value_bias), value_bias])
        query_rows = jnp.dot(flat_in, weight[:, :CHUNK], preferred_element_type=jnp.float32)
        query_rows = ((query_rows + query_bias) * 0.125).astype(jnp.bfloat16)
        pair_rows = jnp.dot(
            seq_in, weight[:, CHUNK : 3 * CHUNK], preferred_element_type=jnp.float32
        )
        pair_rows = (pair_rows + pair_bias).astype(jnp.bfloat16)
        mixed, log = attention_forward(where, query_rows, pair_rows)
        queries.append(query_rows)
        pairs.append(pair_rows)
        attended.append(mixed)
        logs.append(log)

    up_full = later[:, :hidden]
    out_full = later[:, hidden : hidden + width]
    down_full = jnp.stack(
        [
            later[:, begin : begin + width].reshape(device_total, weight_rows, width)
            for begin in range(hidden + width, later.shape[1], width)
        ],
        axis=1,
    ).reshape(hidden, width)

    mixed_low = jnp.concatenate([mixed.astype(jnp.bfloat16) for mixed in attended], axis=1)
    resid_one = (
        flat_in.astype(jnp.float32)
        + jnp.dot(mixed_low, out_full, preferred_element_type=jnp.float32)
        + bias_out
    )
    normed, first_back = jax.vjp(layer_norm, resid_one, gain_one, shift_one)
    normed_low = normed.astype(jnp.bfloat16)
    hidden_pre = jnp.dot(normed_low, up_full, preferred_element_type=jnp.float32) + bias_up
    activated, slope = gelu_parts(hidden_pre)
    hidden_low = activated.astype(jnp.bfloat16)
    resid_two = (
        normed + jnp.dot(hidden_low, down_full, preferred_element_type=jnp.float32) + bias_down
    )
    result, final_back = jax.vjp(layer_norm, resid_two, gain_two, shift_two)
    output = result.astype(jnp.bfloat16).reshape(seq_count, group, width)

    grad_out = cotangent.reshape(group, width).astype(jnp.float32)
    grad_resid_two, final_gain_grad, final_shift_grad = final_back(grad_out)
    grad_down_in = grad_resid_two.astype(jnp.bfloat16)
    down_bias_grad = jnp.sum(grad_down_in.astype(jnp.float32), axis=0)
    down_part = inner_rows(hidden_low, grad_down_in).astype(jnp.bfloat16)
    grad_down_in, down_part = lax.optimization_barrier((grad_down_in, down_part))
    down_share = lax.psum_scatter(
        down_part, ("dp", "ctx"), scatter_dimension=0, tiled=True
    ).astype(jnp.float32)
    grad_hidden = times_transpose(grad_down_in, down_full)
    grad_pre = (grad_hidden * slope).astype(jnp.bfloat16)
    up_bias_grad = jnp.sum(grad_pre.astype(jnp.float32), axis=0)
    up_scatter = Scatter(inner_rows(normed_low, grad_pre), first, bits)
    grad_pre = step_beside(grad_pre, up_scatter)
    grad_normed = grad_resid_two + times_transpose(grad_pre, up_full)
    grad_resid_one, attention_gain_grad, attention_shift_grad = first_back(grad_normed)
    grad_mix_in = grad_resid_one.astype(jnp.bfloat16)
    grad_mix_in = step_beside(grad_mix_in, up_scatter, after=(grad_mix_in,))
    output_bias_grad = jnp.sum(grad_mix_in.astype(jnp.float32), axis=0)
    out_part = inner_rows(mixed_low, grad_mix_in).astype(jnp.bfloat16)
    grad_mix_in, out_part = lax.optimization_barrier((grad_mix_in, out_part))
    grad_mixed = times_transpose(grad_mix_in, out_full).astype(jnp.bfloat16)

    small_grads = [
        output_bias_grad,
        attention_gain_grad,
        attention_shift_grad,
        up_bias_grad,
        down_bias_grad,
        final_gain_grad,
        final_shift_grad,
    ]
    flying = [up_scatter]
    scatters, query_sums, value_sums, spread_back = [], [], [], 0.0
    grad_queries = []
    done = ()
    for chunk in chunks:
        grads = grad_mixed[:, chunk * CHUNK : (chunk + 1) * CHUNK]
        if chunk > 0:
            grads = step_beside(grads, *flying, after=done)
        grad_query, grad_pairs = attention_backward(
            where, queries[chunk], pairs[chunk], attended[chunk], logs[chunk], grads
        )
        spread_back = spread_back + times_transpose(
            grad_pairs, weights[chunk][:, CHUNK : 3 * CHUNK]
        )
        beside = flying
        if chunk == len(chunks) - 1:
            back_scatter = Scatter(spread_back, ctx_bits, ctx_bits[::-1])
            beside = [back_scatter, *flying]
        grad_query, grad_pairs = step_beside(
            (grad_query, grad_pairs), *beside, after=(spread_back,)
        )
        grad_queries.append(grad_query)
        query_sums.append(jnp.sum(grad_query.astype(jnp.float32), axis=0))
        value_sums.append(jnp.sum(grad_pairs[:, CHUNK:].astype(jnp.float32), axis=0))
        parts = [inner_rows(flat_in, grad_query), inner_rows(seq_in, grad_pairs)]
        parts = [part.astype(jnp.bfloat16) for part in parts]
        if chunk == 0:
            parts.append(out_part)
        if chunk == len(chunks) - 1:
            small_grads.insert(0, jnp.concatenate(query_sums + value_sums))
            packed_grads = pack(
                [part.reshape(device_total, size) for part, size in zip(small_grads, widths)],
                weight_rows,
            )
            parts.append(packed_grads.astype(jnp.bfloat16))
        scatter = Scatter(jnp.concatenate(parts, axis=1), orders[chunk % 3], bits)
        if chunk == len(chunks) - 1:
            scatter.held = step_beside(scatter.held, back_scatter, after=(scatter.held,))
        scatters.append(scatter)
        flying = [*flying, scatter]
        done = (spread_back, scatter.held)

    everything = [back_scatter, *flying[::-1]]
    while any(member.todo or member.flying for member in everything):
        for member in everything:
            member.advance()
    own_back = back_scatter.held
    for chunk in chunks:
        own_back = own_back + times_transpose(grad_queries[chunk], weights[chunk][:, :CHUNK])
    input_grad = (grad_resid_one + own_back).reshape(seq_count, group, width)
    shares = [member.held for member in scatters]
    qkv_weight_share = jnp.concatenate(
        [
            share[:, part * CHUNK : (part + 1) * CHUNK]
            for part in range(3)
            for share in shares
        ],
        axis=1,
    )
    output_weight_share = shares[0][:, 3 * CHUNK :]
    pieces = unpack(shares[-1][:, 3 * CHUNK :], widths, weight_rows)
    pieces = [piece.reshape(-1) for piece in pieces]
    (
        qv_bias_share,
        output_bias_share,
        attention_gain_share,
        attention_shift_share,
        up_bias_share,
        down_bias_share,
        final_gain_share,
        final_shift_share,
    ) = pieces
    return (
        output,
        input_grad,
        qkv_weight_share,
        qv_bias_share,
        output_weight_share,
        output_bias_share,
        attention_gain_share,
        attention_shift_share,
        up_scatter.held,
        up_bias_share,
        down_share,
        down_bias_share,
        final_gain_share,
        final_shift_share,
    )


def solution(mesh):
    placed = (
        P("dp", "ctx", None),
        P("dp", None),
        P(("dp", "ctx"), None),
        P(("dp", "ctx")),
        P(("dp", "ctx"), None),
        P(("dp", "ctx")),
        P(("dp", "ctx")),
        P(("dp", "ctx")),
        P(("dp", "ctx"), None),
        P(("dp", "ctx")),
        P(("dp", "ctx"), None),
        P(("dp", "ctx")),
        P(("dp", "ctx")),
        P(("dp", "ctx")),
        P("dp", "ctx", None),
    )
    return jax.shard_map(
        shards,
        mesh=mesh,
        in_specs=placed,
        out_specs=(
            P("dp", "ctx", None),
            P("dp", "ctx", None),
            P(("dp", "ctx"), None),
            P(("dp", "ctx")),
            P(("dp", "ctx"), None),
            P(("dp", "ctx")),
            P(("dp", "ctx")),
            P(("dp", "ctx")),
            P(("dp", "ctx"), None),
            P(("dp", "ctx")),
            P(("dp", "ctx"), None),
            P(("dp", "ctx")),
            P(("dp", "ctx")),
            P(("dp", "ctx")),
        ),
        check_vma=False,
    )
```

```python
import jax
import jax.numpy as jnp
from jax import lax
from jax.experimental import pallas as pl
from jax.experimental.pallas import tpu as pltpu
from jax.sharding import PartitionSpec as P

HEADS = 12
HEAD_DIM = 64
LANES = 128

MASKED = -1000000000.0


def layer_norm(rows, gain, shift):
    center = jnp.mean(rows, axis=-1, keepdims=True)
    centred = rows - center
    spread = jnp.mean(centred * centred, axis=-1, keepdims=True)
    return centred * lax.rsqrt(spread + 1e-06) * gain + shift


def gelu_parts(values):
    below = 0.5 * (1.0 + lax.erf(values * 0.7071067811865476))
    density = 0.3989422804014327 * jnp.exp(-0.5 * values * values)
    return values * below, below + values * density


def inner_rows(left, right):
    return lax.dot_general(
        left, right, (((0,), (0,)), ((), ())), preferred_element_type=jnp.float32
    )


def times_transpose(left, right):
    return lax.dot_general(
        left, right, (((1,), (1,)), ((), ())), preferred_element_type=jnp.float32
    )


def axis_bits(name):
    size = lax.axis_size(name)
    return [(name, 1 << k) for k in range(size.bit_length() - 1)]


def index_bits():
    return axis_bits("dp")[::-1] + axis_bits("ctx")[::-1]


def exchange_orders():
    dp, ctx = axis_bits("dp"), axis_bits("ctx")
    core, side, near, far = ctx[:1], ctx[1:], dp[:1], dp[1:]
    return (
        core + near + side + far,
        core + side + near + far,
        core + far[:1] + near + side + far[1:],
    )


def gather_orders():
    dp, ctx = axis_bits("dp"), axis_bits("ctx")
    core, side, near, far = ctx[:1], ctx[:0:-1], dp[:1], dp[:0:-1]
    return (
        far + near + side + core,
        far[:-1] + near + far[-1:] + side + core,
        far + side + near + core,
    )


def partner(value, bit):
    name, step = bit
    pairs = [(i, i ^ step) for i in range(lax.axis_size(name))]
    return lax.ppermute(value, name, pairs)


def own_bit(bit):
    name, step = bit
    return (lax.axis_index(name) // step) % 2


PAIR = 2 * HEAD_DIM
CHUNK = 2 * PAIR
QUERY_TILE = 256
KEY_TILE = 256


def head_parts(ref, rows):
    lane = lax.broadcasted_iota(jnp.int32, (1, PAIR), 1)
    parts = []
    for begin in range(0, CHUNK, PAIR):
        both = ref[rows, begin : begin + PAIR]
        none = jnp.zeros_like(both)
        parts.append(jnp.where(lane < HEAD_DIM, both, none))
        parts.append(jnp.where(lane < HEAD_DIM, none, both))
    return parts


def forward_kernel(low_ref, high_ref, q_ref, kv_ref, qseg_ref, kseg_ref, o_ref, lse_ref):
    for tile in range(q_ref.shape[0] // QUERY_TILE):
        rows = pl.ds(tile * QUERY_TILE, QUERY_TILE)
        qseg = qseg_ref[tile]
        parts = head_parts(q_ref, rows)

        def step(block, state):
            keys = pl.ds(pl.multiple_of(block * KEY_TILE, KEY_TILE), KEY_TILE)
            allowed = kseg_ref[keys, :] == qseg
            scores = []
            for head, part in enumerate(parts):
                begin = head // 2 * PAIR
                s = lax.dot_general(
                    kv_ref[keys, begin : begin + PAIR],
                    part,
                    (((1,), (1,)), ((), ())),
                    preferred_element_type=jnp.float32,
                )
                scores.append(jnp.where(allowed, s, MASKED))
            tops = [
                jnp.maximum(top, jnp.max(s, axis=0, keepdims=True))
                for s, (top, total, held) in zip(scores, state)
            ]
            weights = [jnp.exp(s - top) for s, top in zip(scores, tops)]
            values = [
                kv_ref[keys, begin : begin + PAIR].T for begin in range(CHUNK, 2 * CHUNK, PAIR)
            ]
            out = []
            for head, (p, new_top, (top, total, held)) in enumerate(zip(weights, tops, state)):
                scale = jnp.exp(top - new_top)
                total = total * scale + jnp.sum(p, axis=0, keepdims=True)
                v_t = values[head // 2][head % 2 * HEAD_DIM : (head % 2 + 1) * HEAD_DIM, :]
                held = held * scale + jnp.dot(
                    v_t, p.astype(jnp.bfloat16), preferred_element_type=jnp.float32
                )
                out.append((new_top, total, held))
            return tuple(out)

        row = jnp.zeros((1, QUERY_TILE), jnp.float32)
        start = (row, row, jnp.zeros((HEAD_DIM, QUERY_TILE), jnp.float32))
        state = lax.fori_loop(low_ref[tile], high_ref[tile], step, (start,) * (CHUNK // HEAD_DIM))
        outs = []
        for head, (top, total, held) in enumerate(state):
            safe = jnp.where(qseg > 0, total, 1.0)
            outs.append(held / safe)
            lse_ref[head : head + 1, rows] = top + jnp.log(safe)
        for pair in range(CHUNK // PAIR):
            both = jnp.concatenate(outs[2 * pair : 2 * pair + 2], axis=0)
            o_ref[rows, pair * PAIR : (pair + 1) * PAIR] = both.T


def backward_kernel(
    low_ref, high_ref, q_ref, kv_ref, qseg_ref, kseg_ref, o_ref, lse_ref, do_ref,
    dq_ref, dkv_ref, sums,
):
    sums[...] = jnp.zeros_like(sums)
    for tile in range(q_ref.shape[0] // QUERY_TILE):
        rows = pl.ds(tile * QUERY_TILE, QUERY_TILE)
        qseg = qseg_ref[tile]
        q_parts = head_parts(q_ref, rows)
        do_parts = head_parts(do_ref, rows)
        deltas = []
        for begin in range(0, CHUNK, PAIR):
            do = do_ref[rows, begin : begin + PAIR].astype(jnp.float32)
            prod_t = (do * o_ref[rows, begin : begin + PAIR]).T
            deltas.append(jnp.sum(prod_t[:HEAD_DIM, :], axis=0, keepdims=True))
            deltas.append(jnp.sum(prod_t[HEAD_DIM:, :], axis=0, keepdims=True))
        logs = [lse_ref[head : head + 1, rows] for head in range(CHUNK // HEAD_DIM)]

        def step(block, state):
            keys = pl.ds(pl.multiple_of(block * KEY_TILE, KEY_TILE), KEY_TILE)
            allowed = kseg_ref[keys, :] == qseg
            heads = range(CHUNK // HEAD_DIM)
            ks = [kv_ref[keys, begin : begin + PAIR] for begin in range(0, CHUNK, PAIR)]
            vs = [kv_ref[keys, begin : begin + PAIR] for begin in range(CHUNK, 2 * CHUNK, PAIR)]
            scores = [
                lax.dot_general(
                    ks[head // 2],
                    q_parts[head],
                    (((1,), (1,)), ((), ())),
                    preferred_element_type=jnp.float32,
                )
                for head in heads
            ]
            slopes = [
                lax.dot_general(
                    vs[head // 2],
                    do_parts[head],
                    (((1,), (1,)), ((), ())),
                    preferred_element_type=jnp.float32,
                )
                for head in heads
            ]
            probs = [
                jnp.exp(jnp.where(allowed, scores[head], MASKED) - logs[head]) for head in heads
            ]
            lows = [p.astype(jnp.bfloat16) for p in probs]
            grads = [
                (probs[head] * (slopes[head] - deltas[head])).astype(jnp.bfloat16) for head in heads
            ]
            k_ts = [k.T for k in ks]
            out = []
            for pair in range(CHUNK // PAIR):
                begin = pair * PAIR
                dk, dv = 0.0, 0.0
                for side in range(2):
                    head = 2 * pair + side
                    dv += jnp.dot(lows[head], do_parts[head], preferred_element_type=jnp.float32)
                    dk += jnp.dot(grads[head], q_parts[head], preferred_element_type=jnp.float32)
                    out.append(
                        state[head]
                        + jnp.dot(
                            k_ts[pair][side * HEAD_DIM : (side + 1) * HEAD_DIM, :],
                            grads[head],
                            preferred_element_type=jnp.float32,
                        )
                    )
                sums[keys, begin : begin + PAIR] += dk
                sums[keys, CHUNK + begin : CHUNK + begin + PAIR] += dv
            return tuple(out)

        start = jnp.zeros((HEAD_DIM, QUERY_TILE), jnp.float32)
        state = lax.fori_loop(low_ref[tile], high_ref[tile], step, (start,) * (CHUNK // HEAD_DIM))
        for pair in range(CHUNK // PAIR):
            both = jnp.concatenate(state[2 * pair : 2 * pair + 2], axis=0)
            dq_ref[rows, pair * PAIR : (pair + 1) * PAIR] = (both.T * 0.125).astype(jnp.bfloat16)
    dkv_ref[...] = sums[...].astype(jnp.bfloat16)


def key_ranges(query_seg, seg_row):
    tiles = query_seg.reshape(-1, QUERY_TILE)
    first = tiles[:, 0]
    last = jnp.max(tiles, axis=1)
    real = seg_row > 0
    before = jnp.sum((real & (seg_row < first[:, None])).astype(jnp.int32), axis=1)
    until = jnp.sum((real & (seg_row <= last[:, None])).astype(jnp.int32), axis=1)
    low = before // KEY_TILE
    high = (until + KEY_TILE - 1) // KEY_TILE
    return jnp.where(first > 0, low, 0), jnp.where(first > 0, high, 0)


def whole_block(shape):
    return pl.BlockSpec(shape, lambda step, low, high: (0,) * len(shape))


def attention_call(kernel, name, where, operands, out_shape, scratch, matmuls):
    group = operands[0].shape[0]
    low, high, query_ids, key_ids = where
    queries, pairs = operands[:2]
    operands = [queries, pairs, query_ids, key_ids, *operands[2:]]
    return pl.pallas_call(
        kernel,
        grid_spec=pltpu.PrefetchScalarGridSpec(
            num_scalar_prefetch=2,
            grid=(1,),
            in_specs=[whole_block(operand.shape) for operand in operands],
            out_specs=[whole_block(member.shape) for member in out_shape],
            scratch_shapes=scratch,
        ),
        out_shape=out_shape,
        compiler_params=pltpu.CompilerParams(vmem_limit_bytes=40 << 20),
        cost_estimate=pl.CostEstimate(
            flops=matmuls * group * CHUNK, bytes_accessed=group * CHUNK, transcendentals=0
        ),
        name=name,
    )(low, high, *operands)


def attention_forward(where, queries, pairs):
    group = queries.shape[0]
    out_shape = [
        jax.ShapeDtypeStruct((group, CHUNK), jnp.float32),
        jax.ShapeDtypeStruct((CHUNK // HEAD_DIM, group), jnp.float32),
    ]
    return attention_call(
        forward_kernel, "attention_forward", where, [queries, pairs], out_shape, [], 2
    )


def attention_backward(where, queries, pairs, attended, logs, grad_mixed):
    group, seq_len = queries.shape[0], pairs.shape[0]
    out_shape = [
        jax.ShapeDtypeStruct((group, CHUNK), jnp.bfloat16),
        jax.ShapeDtypeStruct((seq_len, 2 * CHUNK), jnp.bfloat16),
    ]
    return attention_call(
        backward_kernel,
        "attention_backward",
        where,
        [queries, pairs, attended, logs, grad_mixed],
        out_shape,
        [pltpu.VMEM((seq_len, 2 * CHUNK), jnp.float32)],
        5,
    )


class Exchange:
    def __init__(self, held, order, bits):
        self.held, self.todo, self.bits = held, list(order), bits
        self.flying = None

    def finish(self, *after):
        if self.flying is None:
            return
        bit, keep, theirs = self.flying
        self.flying = None
        if after:
            theirs = lax.optimization_barrier((theirs, *after))[0]
        self.merge(bit, keep, theirs)

    def advance(self, *after):
        self.finish(*after)
        if self.todo:
            bit = self.todo.pop(0)
            keep, send = self.split(bit)
            self.flying = bit, keep, partner(send, bit)

    def run(self, steps=None):
        for step in range(len(self.todo) if steps is None else steps):
            self.advance()
            self.finish()
        return self


class Gather(Exchange):
    def __init__(self, shard, order, bits):
        super().__init__(shard, order, bits)
        self.rows, self.cols = shard.shape
        self.have = []

    def split(self, bit):
        return self.held, self.held

    def merge(self, bit, keep, theirs):
        place = sum(1 for other in self.have if self.bits.index(other) < self.bits.index(bit))
        shape = [1] * (keep.ndim + 1)
        shape[place] = 2
        mine = jnp.arange(2).reshape(shape) == own_bit(bit)
        self.held = jnp.where(mine, jnp.expand_dims(keep, place), jnp.expand_dims(theirs, place))
        self.have.append(bit)

    def full(self):
        return self.held.reshape(self.rows << len(self.have), self.cols)


class Scatter(Exchange):
    def __init__(self, full, order, bits):
        rows, cols = full.shape
        shape = [2] * len(bits) + [rows >> len(bits), cols]
        super().__init__(full.astype(jnp.bfloat16).reshape(shape), order, bits)
        self.have = list(bits)

    def split(self, bit):
        place = self.have.index(bit)
        mine = own_bit(bit)
        keep = lax.dynamic_index_in_dim(self.held, mine, place, keepdims=False)
        send = lax.dynamic_index_in_dim(self.held, 1 - mine, place, keepdims=False)
        return keep, send

    def merge(self, bit, keep, theirs):
        total = keep.astype(jnp.float32) + theirs.astype(jnp.float32)
        self.have.remove(bit)
        self.held = total.astype(jnp.bfloat16) if self.have else total


def spots(count, rows):
    places = [(k % rows, k // rows * LANES) for k in range(count)]
    return places, (count + rows - 1) // rows * LANES


def pack(members, rows):
    places, columns = spots(len(members), rows)
    total = 0
    for member, (row, column) in zip(members, places):
        count, size = member.shape
        edges = ((0, 0), (row, rows - 1 - row), (column, columns - column - size))
        total = total + jnp.pad(member[:, None, :], edges)
    return total.reshape(-1, columns)


def unpack(packed, widths, rows):
    places, columns = spots(len(widths), rows)
    blocks = packed.reshape(-1, rows, columns)
    return [
        blocks[:, row, column : column + size]
        for (row, column), size in zip(places, widths)
    ]


def hold(value, *exchanges):
    held = lax.optimization_barrier((value, *[member.held for member in exchanges]))
    for member, new in zip(exchanges, held[1:]):
        member.held = new
    return held[0]


def step_beside(value, *exchanges, after=()):
    for member in exchanges:
        member.finish(*after)
    value = hold(value, *exchanges)
    for member in exchanges:
        member.advance()
    return value


def shards(
    inputs,
    segments,
    qkv_weight,
    query_value_bias,
    output_weight,
    output_bias,
    attention_gain,
    attention_shift,
    up_weight,
    up_bias,
    down_weight,
    down_bias,
    final_gain,
    final_shift,
    cotangent,
):
    seq_count, group, width = inputs.shape
    seq_len = segments.shape[1]
    device_total = lax.axis_size("dp") * lax.axis_size("ctx")
    bits = index_bits()
    ctx_bits = axis_bits("ctx")
    first, second, third = orders = exchange_orders()
    flat_in = inputs.reshape(group, width)
    seg_row = segments.reshape(seq_len)
    chunks = range(width // CHUNK)

    small = (
        query_value_bias,
        output_bias,
        attention_gain,
        attention_shift,
        up_bias,
        down_bias,
        final_gain,
        final_shift,
    )
    widths = [member.shape[0] for member in small]
    weight_rows = qkv_weight.shape[0]
    packed = pack([member[None, :] for member in small], weight_rows)

    later = lax.all_gather(
        jnp.concatenate([up_weight, output_weight], axis=1), ("dp", "ctx"), axis=0, tiled=True
    )
    hidden = up_weight.shape[1]

    seq_gather = Gather(flat_in, ctx_bits[::-1], ctx_bits[::-1])
    gathers = []
    for chunk in chunks:
        parts = [
            qkv_weight[:, base + chunk * CHUNK : base + (chunk + 1) * CHUNK]
            for base in (0, width, 2 * width)
        ]
        if chunk == 0:
            parts.append(packed)
        gathers.append(Gather(jnp.concatenate(parts, axis=1), gather_orders()[chunk % 3], bits))
    seq_gather.run(len(ctx_bits) - 2)
    seq_gather.advance()
    for member in gathers:
        member.run(len(bits) - 2)
    seq_gather.advance(*[member.held for member in gathers])
    down_gather = Gather(hold(down_weight, *gathers), gather_orders()[2], bits)
    down_gather.run(len(bits) - 4)
    down_gather.advance()
    for member in gathers:
        member.run()
    seq_gather.finish()
    seq_in = seq_gather.full()
    weights = [member.full() for member in gathers]
    members = unpack(weights[0][:, 3 * CHUNK :], widths, weight_rows)
    members = [member.reshape(-1).astype(jnp.float32) for member in members]
    bias_qv, bias_out, gain_one, shift_one, bias_up, bias_down, gain_two, shift_two = members

    offset = lax.axis_index("ctx") * group
    query_seg = lax.dynamic_slice_in_dim(seg_row, offset, group, 0)
    query_ids = jnp.where(query_seg > 0, query_seg, -1).reshape(-1, 1, QUERY_TILE)
    where = (*key_ranges(query_seg, seg_row), query_ids, seg_row[:, None])

    queries, pairs, attended, logs = [], [], [], []
    for chunk in chunks:
        begin = chunk * CHUNK
        weight = weights[chunk]
        query_bias = bias_qv[begin : begin + CHUNK]
        value_bias = bias_qv[width + begin : width + begin + CHUNK]
        pair_bias = jnp.concatenate([jnp.zeros_like(value_bias), value_bias])
        query_rows = jnp.dot(flat_in, weight[:, :CHUNK], preferred_element_type=jnp.float32)
        query_rows = ((query_rows + query_bias) * 0.125).astype(jnp.bfloat16)
        pair_rows = jnp.dot(
            seq_in, weight[:, CHUNK : 3 * CHUNK], preferred_element_type=jnp.float32
        )
        pair_rows = (pair_rows + pair_bias).astype(jnp.bfloat16)
        if chunk == 0:
            query_rows = step_beside(query_rows, down_gather, after=(query_rows,))
        if chunk == len(chunks) - 1:
            query_rows = step_beside(query_rows, down_gather, after=(logs[-1],))
        mixed, log = attention_forward(where, query_rows, pair_rows)
        queries.append(query_rows)
        pairs.append(pair_rows)
        attended.append(mixed)
        logs.append(log)

    up_full = later[:, :hidden]
    out_full = later[:, hidden:]

    mixed_low = jnp.concatenate([mixed.astype(jnp.bfloat16) for mixed in attended], axis=1)
    resid_one = (
        flat_in.astype(jnp.float32)
        + jnp.dot(mixed_low, out_full, preferred_element_type=jnp.float32)
        + bias_out
    )
    normed, first_back = jax.vjp(layer_norm, resid_one, gain_one, shift_one)
    normed_low = normed.astype(jnp.bfloat16)
    hidden_pre = jnp.dot(normed_low, up_full, preferred_element_type=jnp.float32) + bias_up
    activated, slope = gelu_parts(hidden_pre)
    hidden_low = activated.astype(jnp.bfloat16)
    down_gather.finish(resid_one)
    hidden_pre = hold(hidden_pre, down_gather)
    down_gather.run()
    down_full = down_gather.full()
    resid_two = (
        normed + jnp.dot(hidden_low, down_full, preferred_element_type=jnp.float32) + bias_down
    )
    result, final_back = jax.vjp(layer_norm, resid_two, gain_two, shift_two)
    output = result.astype(jnp.bfloat16).reshape(seq_count, group, width)

    grad_out = cotangent.reshape(group, width).astype(jnp.float32)
    grad_resid_two, final_gain_grad, final_shift_grad = final_back(grad_out)
    grad_down_in = grad_resid_two.astype(jnp.bfloat16)
    down_bias_grad = jnp.sum(grad_down_in.astype(jnp.float32), axis=0)
    down_part = inner_rows(hidden_low, grad_down_in).astype(jnp.bfloat16)
    grad_down_in, down_part = lax.optimization_barrier((grad_down_in, down_part))
    down_share = lax.psum_scatter(
        down_part, ("dp", "ctx"), scatter_dimension=0, tiled=True
    ).astype(jnp.float32)
    grad_hidden = times_transpose(grad_down_in, down_full)
    grad_pre = (grad_hidden * slope).astype(jnp.bfloat16)
    up_bias_grad = jnp.sum(grad_pre.astype(jnp.float32), axis=0)
    up_scatter = Scatter(inner_rows(normed_low, grad_pre), first, bits)
    grad_pre = step_beside(grad_pre, up_scatter)
    grad_normed = grad_resid_two + times_transpose(grad_pre, up_full)
    grad_resid_one, attention_gain_grad, attention_shift_grad = first_back(grad_normed)
    grad_mix_in = grad_resid_one.astype(jnp.bfloat16)
    grad_mix_in = step_beside(grad_mix_in, up_scatter, after=(grad_mix_in,))
    output_bias_grad = jnp.sum(grad_mix_in.astype(jnp.float32), axis=0)
    out_part = inner_rows(mixed_low, grad_mix_in).astype(jnp.bfloat16)
    grad_mix_in, out_part = lax.optimization_barrier((grad_mix_in, out_part))
    grad_mixed = times_transpose(grad_mix_in, out_full).astype(jnp.bfloat16)

    small_grads = [
        output_bias_grad,
        attention_gain_grad,
        attention_shift_grad,
        up_bias_grad,
        down_bias_grad,
        final_gain_grad,
        final_shift_grad,
    ]
    flying = [up_scatter]
    scatters, query_sums, value_sums, spread_back = [], [], [], 0.0
    grad_queries = []
    done = ()
    for chunk in chunks:
        grads = grad_mixed[:, chunk * CHUNK : (chunk + 1) * CHUNK]
        if chunk > 0:
            grads = step_beside(grads, *flying, after=done)
        grad_query, grad_pairs = attention_backward(
            where, queries[chunk], pairs[chunk], attended[chunk], logs[chunk], grads
        )
        if chunk < len(chunks) - 1:
            spread_back = spread_back + times_transpose(
                grad_pairs, weights[chunk][:, CHUNK : 3 * CHUNK]
            )
        beside = flying if chunk > 0 else []
        last = chunk == len(chunks) - 1
        grad_query, grad_pairs = step_beside(
            (grad_query, grad_pairs), *beside, after=(grad_query if last else spread_back,)
        )
        grad_queries.append(grad_query)
        query_sums.append(jnp.sum(grad_query.astype(jnp.float32), axis=0))
        value_sums.append(jnp.sum(grad_pairs[:, CHUNK:].astype(jnp.float32), axis=0))
        parts = [inner_rows(flat_in, grad_query), inner_rows(seq_in, grad_pairs)]
        parts = [part.astype(jnp.bfloat16) for part in parts]
        if chunk == 0:
            parts.append(out_part)
        if chunk == len(chunks) - 1:
            small_grads.insert(0, jnp.concatenate(query_sums + value_sums))
            packed_grads = pack(
                [part.reshape(device_total, size) for part, size in zip(small_grads, widths)],
                weight_rows,
            )
            parts.append(packed_grads.astype(jnp.bfloat16))
        scatter = Scatter(jnp.concatenate(parts, axis=1), orders[chunk % 3], bits)
        if last:
            grad_pairs = step_beside(grad_pairs, scatter)
            spread_back = spread_back + times_transpose(
                grad_pairs, weights[chunk][:, CHUNK : 3 * CHUNK]
            )
            back_scatter = Scatter(spread_back, ctx_bits, ctx_bits[::-1])
        scatters.append(scatter)
        flying = [*flying, scatter]
        done = (spread_back, scatter.held)

    final = scatters[-1]
    for step in range(len(bits)):
        for member in flying[:-1]:
            member.advance()
        final.finish()
        if step == 0:
            final.held = step_beside(final.held, back_scatter)
        if step == 2:
            back_scatter.finish(final.held)
            back_scatter.run()
            final.held = hold(final.held, back_scatter)
        final.advance()
    for member in flying:
        member.finish()
        member.run()
    own_back = back_scatter.held
    for chunk in chunks:
        own_back = own_back + times_transpose(grad_queries[chunk], weights[chunk][:, :CHUNK])
    input_grad = (grad_resid_one + own_back).reshape(seq_count, group, width)
    shares = [member.held for member in scatters]
    qkv_weight_share = jnp.concatenate(
        [
            share[:, part * CHUNK : (part + 1) * CHUNK]
            for part in range(3)
            for share in shares
        ],
        axis=1,
    )
    output_weight_share = shares[0][:, 3 * CHUNK :]
    pieces = unpack(shares[-1][:, 3 * CHUNK :], widths, weight_rows)
    pieces = [piece.reshape(-1) for piece in pieces]
    (
        qv_bias_share,
        output_bias_share,
        attention_gain_share,
        attention_shift_share,
        up_bias_share,
        down_bias_share,
        final_gain_share,
        final_shift_share,
    ) = pieces
    return (
        output,
        input_grad,
        qkv_weight_share,
        qv_bias_share,
        output_weight_share,
        output_bias_share,
        attention_gain_share,
        attention_shift_share,
        up_scatter.held,
        up_bias_share,
        down_share,
        down_bias_share,
        final_gain_share,
        final_shift_share,
    )


def solution(mesh):
    placed = (
        P("dp", "ctx", None),
        P("dp", None),
        P(("dp", "ctx"), None),
        P(("dp", "ctx")),
        P(("dp", "ctx"), None),
        P(("dp", "ctx")),
        P(("dp", "ctx")),
        P(("dp", "ctx")),
        P(("dp", "ctx"), None),
        P(("dp", "ctx")),
        P(("dp", "ctx"), None),
        P(("dp", "ctx")),
        P(("dp", "ctx")),
        P(("dp", "ctx")),
        P("dp", "ctx", None),
    )
    return jax.shard_map(
        shards,
        mesh=mesh,
        in_specs=placed,
        out_specs=(
            P("dp", "ctx", None),
            P("dp", "ctx", None),
            P(("dp", "ctx"), None),
            P(("dp", "ctx")),
            P(("dp", "ctx"), None),
            P(("dp", "ctx")),
            P(("dp", "ctx")),
            P(("dp", "ctx")),
            P(("dp", "ctx"), None),
            P(("dp", "ctx")),
            P(("dp", "ctx"), None),
            P(("dp", "ctx")),
            P(("dp", "ctx")),
            P(("dp", "ctx")),
        ),
        check_vma=False,
    )
```
